512 devices in a mesh: ctx: 128 (over x, z, core), head: 4 (over y).
Axes of the slice: x: 4, y: 4, z: 16, core: 2. Of those that a mesh axis runs over, the one named last changes fastest.
Arguments:
- queries: bfloat16 [4, 16384, 1024], P(None, 'ctx', 'head'), may hold values from -45 to 45
- keys: bfloat16 [4, 16384, 1024], P(None, 'ctx', 'head'), may hold values from -6 to 6
- values: bfloat16 [4, 16384, 1024], P(None, 'ctx', 'head'), may hold values from -6 to 6
- out_weight: bfloat16 [1024, 2048], P(None, 'head'), may hold values from -0.1875 to 0.1875
- global_ids: int32 [4, 2], replicated, may hold values from 0 to 255, as said below
- rand_ids: int32 [4, 256, 4], P(None, 'ctx'), may hold values from 0 to 255, as said below
- rand_count: int32 [4, 256], P(None, 'ctx'), may hold values from 1 to 4
Outputs:
- output: bfloat16 [4, 16384, 2048], P(None, 'ctx', 'head')
The draws below stay inside these ranges and needn't reach their ends.
Inputs may be any that keep to these rules, and one draw needn't show every extreme that they name: `global_ids`: block ids; the 2 ids of one sequence are distinct. `rand_ids`: block ids of the same sequence. Taking together the 2 query blocks that each of the 4 sequences has on one index of ctx, at most 1 live slots name blocks held by any one index of ctx.
All inputs are finite; a program needn't handle non-finite values.
Results may differ from the reference program's by a relative error of at most 0.0056.
Values may be sent and summed in bfloat16 or wider, within the bound.
A program may use at most 64 MiB of HBM per device.

```python
import jax
import jax.numpy as jnp
from jax import lax

D = 2048
HEADS = 8
HEAD_DIM = 128
BLOCK = 64
GLOB = 2
RMAX = 4
SEQ_DEV = 128
SEQS = 4
LEN = 16384
NB = 256
HW = 1024


def query_key_pair(key):
    folded = jax.random.fold_in(key, 7)
    key_query, key_keys = jax.random.split(folded, 2)
    full_shape = (SEQS, LEN, HEADS * HEAD_DIM)
    query_vals = jnp.clip(jax.random.normal(key_query, full_shape, jnp.float32), -6.0, 6.0)
    key_vals = jnp.clip(jax.random.normal(key_keys, full_shape, jnp.float32), -6.0, 6.0)
    return (query_vals, key_vals)


def draw_queries(key, part):
    return query_key_pair(key)[0].astype(jnp.bfloat16)


def draw_keys(key, part):
    return query_key_pair(key)[1].astype(jnp.bfloat16)


def draw_global_ids(key, part):
    folded = jax.random.fold_in(key, 23)
    orders = jax.vmap(lambda single: jax.random.permutation(single, NB))(jax.random.split(folded, SEQS))
    chosen = orders[:, :GLOB]
    edge_ids = jnp.where(jnp.arange(GLOB) == 0, NB - 1, jnp.where(jnp.arange(GLOB) == 1, 0, chosen[0]))
    edge_clash = (chosen[0][:, None] == jnp.array([NB - 1, 0])[None, :]).any(axis=1) & (jnp.arange(GLOB) >= 2)
    fallback = jnp.arange(GLOB) + 1
    first_row = jnp.where(edge_clash, fallback, edge_ids)
    chosen = jnp.where((jnp.arange(SEQS) == 0)[:, None], first_row[None, :], chosen)
    return chosen.astype(jnp.int32)


def block_lists(key):
    folded = jax.random.fold_in(key, 19)
    key_perm, key_within, key_heavy, key_forced, key_light = jax.random.split(folded, 5)
    devices = LEN // SEQ_DEV
    per_device = SEQ_DEV // BLOCK
    request_total = SEQS * per_device * RMAX
    orders = jax.vmap(lambda single: jax.random.permutation(single, devices))(jax.random.split(key_perm, devices))
    ascending = jnp.arange(devices, dtype=orders.dtype)
    orders = orders.at[0].set(devices - 1 - ascending)
    orders = orders.at[1].set(ascending)
    owners = orders[:, jnp.arange(request_total) % devices]
    within = jax.random.randint(key_within, (devices, request_total), 0, per_device)
    within = within.at[0, 0].set(per_device - 1)
    within = within.at[1, 0].set(0)
    block_ids = (owners * per_device + within).reshape(devices, SEQS, per_device, RMAX)
    block_ids = jnp.transpose(block_ids, (1, 0, 2, 3)).reshape(SEQS, devices * per_device, RMAX)
    heavy_dev = jax.random.randint(key_heavy, (devices,), 0, 8) == 0
    forced = jax.random.randint(key_forced, (), 0, devices)
    heavy_dev = heavy_dev | (jnp.arange(devices) == forced)
    light_counts = jax.random.randint(key_light, (SEQS, devices, per_device), 1, RMAX)
    live_counts = jnp.where(heavy_dev[None, :, None], RMAX, light_counts).reshape(SEQS, devices * per_device)
    return (block_ids.astype(jnp.int32), live_counts.astype(jnp.int32))


def draw_rand_ids(key, part):
    return block_lists(key)[0]


def draw_rand_count(key, part):
    return block_lists(key)[1]


def shard_levels(stream_key, extent, cuts, low, largest):
    level, own = 1.0, jax.random.fold_in(stream_key, 6)
    for axis_at, parts in cuts:
        heights = jnp.exp(jax.random.uniform(jax.random.fold_in(own, axis_at), (parts,), jnp.float32, low / len(cuts), largest / len(cuts)))
        level = level * jnp.repeat(heights, extent[axis_at] // parts).reshape([-1 if axis == axis_at else 1 for axis in range(len(extent))])
    return level


def scatter_about(own_key, dims, spread, most, cuts=(), held_as=jnp.bfloat16):
    values = spread * jax.random.normal(own_key, dims, jnp.float32)
    if cuts:
        values = values * shard_levels(own_key, dims, cuts, -0.22, 0.18)
    return jnp.clip(values, -most, most).astype(held_as)


def setup_inputs(seed: int = 0) -> dict:
    arg_keys = jax.random.split(jax.random.key(seed), 8)
    return {
        "queries": draw_queries(jax.random.fold_in(arg_keys[7], 71), 0),
        "keys": draw_keys(jax.random.fold_in(arg_keys[7], 71), 0),
        "values": scatter_about(arg_keys[2], (SEQS, LEN, HW), 1.0, 6.0, ((1, 128), (2, 4))),
        "out_weight": scatter_about(arg_keys[3], (HW, D), HW ** -0.5, 0.1875, ((1, 4),)),
        "global_ids": draw_global_ids(jax.random.fold_in(arg_keys[7], 71), 0),
        "rand_ids": draw_rand_ids(jax.random.fold_in(arg_keys[7], 71), 0),
        "rand_count": draw_rand_count(jax.random.fold_in(arg_keys[7], 71), 0),
    }


def attend_block(query_block, key_rows, value_rows, live_cols):
    score_scale = HEAD_DIM ** -0.5
    scores = jnp.einsum("qhd,khd->hqk", query_block.astype(jnp.float32), key_rows.astype(jnp.float32)) * score_scale
    masked = jnp.where(live_cols[None, None, :], scores, -1e30)
    row_peak = jnp.max(masked, axis=-1, keepdims=True)
    weights = jnp.where(live_cols[None, None, :], jnp.exp(masked - row_peak), 0.0)
    row_total = jnp.sum(weights, axis=-1)
    rounded = lax.optimization_barrier(weights.astype(jnp.bfloat16)).astype(jnp.float32)
    weighted = jnp.einsum("hqk,khd->qhd", rounded, value_rows.astype(jnp.float32))
    return (weighted / jnp.transpose(row_total)[:, :, None]).astype(jnp.bfloat16)


def reference(queries, keys, values, out_weight, global_ids, rand_ids, rand_count):
    block_count = queries.shape[1] // BLOCK
    outputs = []
    for seq_index in range(SEQS):
        query_blocks = queries[seq_index].reshape(block_count, BLOCK, HEADS, HEAD_DIM)
        key_blocks = keys[seq_index].reshape(block_count, BLOCK, HEADS, HEAD_DIM)
        value_blocks = values[seq_index].reshape(block_count, BLOCK, HEADS, HEAD_DIM)
        shared_ids = global_ids[seq_index].astype(jnp.int32)

        def one_block(operands, query_blocks=query_blocks, key_blocks=key_blocks, value_blocks=value_blocks, shared_ids=shared_ids):
            block_index, listed, listed_count = operands
            window_ids = jnp.stack([(block_index - 1) % block_count, block_index, (block_index + 1) % block_count]).astype(jnp.int32)
            chosen = jnp.concatenate([window_ids, shared_ids, listed.astype(jnp.int32)])
            key_rows = jnp.take(key_blocks, chosen, axis=0).reshape(-1, HEADS, HEAD_DIM)
            value_rows = jnp.take(value_blocks, chosen, axis=0).reshape(-1, HEADS, HEAD_DIM)
            live_slots = jnp.concatenate([jnp.ones((3 + GLOB,), jnp.bool_), jnp.arange(RMAX, dtype=jnp.int32) < listed_count])
            live_cols = jnp.repeat(live_slots, BLOCK)
            return attend_block(jnp.take(query_blocks, block_index, axis=0), key_rows, value_rows, live_cols)

        attended = lax.map(one_block, (jnp.arange(block_count, dtype=jnp.int32), rand_ids[seq_index], rand_count[seq_index]))
        flattened = attended.reshape(block_count * BLOCK, HEADS * HEAD_DIM)
        outputs.append(jnp.dot(flattened, out_weight, preferred_element_type=jnp.float32).astype(jnp.bfloat16))
    return jnp.stack(outputs)
```

```python
import jax
import jax.numpy as jnp
from jax import lax
from jax.experimental import pallas as pl
from jax.experimental.pallas import tpu as pltpu
from jax.sharding import PartitionSpec as P

HEAD_DIM = 128
BLOCK = 64
GLOB = 2
RMAX = 4
NX, NZ, NC = 4, 16, 2
ROW = NX * NC
SEQS = 4
BPD = 2
OWN = SEQS * BPD
CAP = 16
PAIRS = 4
HALF = OWN // 2
MESH = pl.DeviceIdType.MESH


def exchange_kernel(
    kb, vb, req, gcode, gown, rcv, glob, halo_k, halo_v,
    gath0, gath1, gath2, gath3, offer0, offer1, offer2, offer3, pack, cand, pick, req_in, req_s,
    own_sem, z_send, z_recv, x_send, x_recv, c_send, c_recv, g_send, g_recv,
    h_send, h_recv, r_send, r_recv, s_sem, gl_sem,
):
    gath = (gath0, gath1, gath2, gath3)
    cand_in = (offer0, offer1, offer2, offer3)
    ctx = lax.axis_index("ctx")
    head = lax.axis_index("head")
    x, z, c = ctx // (NZ * NC), (ctx // NC) % NZ, ctx % NC
    me = x * NC + c

    def at_z(step):
        return (x * (NZ * NC) + ((z + step + NZ) % NZ) * NC + c, head)

    def at_row(r):
        return ((r // NC) * (NZ * NC) + z * NC + r % NC, head)

    count = NX * NZ * NC
    right = ((ctx + 1) % count, head)
    left = ((ctx + count - 1) % count, head)

    own = [
        pltpu.make_async_copy(
            (kb, vb)[p % 2].at[:, :, pl.ds((p // 2) * HEAD_DIM, HEAD_DIM)],
            gath[p].at[pl.ds(0, OWN)],
            own_sem.at[p],
        )
        for p in range(PAIRS)
    ]
    for copy in own:
        copy.start()
    own_req = pltpu.make_async_copy(req.at[0], req_s.at[0], s_sem.at[0])
    own_req.start()

    barrier = pltpu.get_barrier_semaphore()
    peers = [at_z(1), at_z(-1), right, left] + [at_row((me + k) % ROW) for k in range(1, ROW)]
    for peer in peers:
        pl.semaphore_signal(barrier, inc=1, device_id=peer, device_id_type=MESH)
    pl.semaphore_wait(barrier, len(peers))

    def req_copy(k):
        return pltpu.make_async_remote_copy(
            src_ref=req.at[k], dst_ref=req_in.at[k],
            send_sem=r_send.at[k], recv_sem=r_recv.at[k],
            device_id=at_row((me + ROW - k) % ROW), device_id_type=MESH,
        )

    for k in range(1, ROW):
        req_copy(k).start()

    def z_copy(p, way, t, a):
        if way == 0:
            src, dst, peer = (-t) % NZ, (-t - 1) % NZ, at_z(1)
        else:
            src, dst, peer = t, t + 1, at_z(-1)
        return pltpu.make_async_remote_copy(
            src_ref=gath[p].at[pl.ds(src * OWN + a * HALF, HALF)],
            dst_ref=gath[p].at[pl.ds(dst * OWN + a * HALF, HALF)],
            send_sem=z_send.at[p, (way * 8 + t) * 2 + a],
            recv_sem=z_recv.at[p, (way * 8 + t) * 2 + a],
            device_id=peer, device_id_type=MESH,
        )

    def used(way, t, a):
        return t < 7 or a == way

    def z_first(p):
        for a in range(2):
            for way in range(2):
                z_copy(p, way, 0, a).start()

    for copy in own:
        copy.wait()
    z_first(0)

    halos = []
    for i, (src, dst) in enumerate(((kb, halo_k), (vb, halo_v))):
        for side in range(2):
            halos.append(
                [
                    pltpu.make_async_remote_copy(
                        src_ref=src.at[2 * s + 1 - side], dst_ref=dst.at[side, s],
                        send_sem=h_send.at[(i * 2 + side) * SEQS + s],
                        recv_sem=h_recv.at[(i * 2 + side) * SEQS + s],
                        device_id=(right, left)[side], device_id_type=MESH,
                    )
                    for s in range(SEQS)
                ]
            )
    for group in halos:
        for copy in group:
            copy.start()

    own_req.wait()
    for k in range(1, ROW):
        req_copy(k).wait()
    rest = [
        pltpu.make_async_copy(req_in.at[k], req_s.at[k], s_sem.at[k]) for k in range(1, ROW)
    ]
    for copy in rest:
        copy.start()
    for copy in rest:
        copy.wait()

    def x_copy(p, k):
        return pltpu.make_async_remote_copy(
            src_ref=pack.at[p, k], dst_ref=rcv.at[p, k],
            send_sem=x_send.at[p, k], recv_sem=x_recv.at[p, k],
            device_id=at_row((me + k) % ROW), device_id_type=MESH,
        )

    def c_copy(p, k):
        return pltpu.make_async_remote_copy(
            src_ref=cand.at[p, k], dst_ref=cand_in[p].at[k],
            send_sem=c_send.at[p, k], recv_sem=c_recv.at[p, k],
            device_id=at_row((me + k) % ROW), device_id_type=MESH,
        )

    def g_copy(p, k):
        return pltpu.make_async_remote_copy(
            src_ref=pick.at[p], dst_ref=glob.at[p, k],
            send_sem=g_send.at[p, k], recv_sem=g_recv.at[p, k],
            device_id=at_row((me + k) % ROW), device_id_type=MESH,
        )

    def self_copies(p):
        return (
            pltpu.make_async_copy(pack.at[p, 0], rcv.at[p, 0], x_send.at[p, 0]),
            pltpu.make_async_copy(pick.at[p], glob.at[p, 0], g_send.at[p, 0]),
        )

    def one_pair(p):
        for t in range(1, 8):
            for a in range(2):
                for way in range(2):
                    z_copy(p, way, t - 1, a).wait_recv()
                    if used(way, t, a):
                        z_copy(p, way, t, a).start()
        for way in range(2):
            z_copy(p, way, 7, way).wait_recv()

        if p < PAIRS - 1:
            z_first(p + 1)

        def offer(k, carry):
            cand[p, k] = gath[p][gcode[(me + k) % ROW]]

            @pl.when(k > 0)
            def _():
                c_copy(p, k).start()

            return carry

        lax.fori_loop(0, ROW, offer, 0)
        cand_in[p][0] = cand[p, 0]

        def fill(k, carry):
            for n in range(CAP):
                pack[p, k, n] = gath[p][req_s[k, 0, n]]

            @pl.when(k > 0)
            def _():
                x_copy(p, k).start()

            return carry

        lax.fori_loop(0, ROW, fill, 0)

        def landed(k, carry):
            c_copy(p, k).wait_recv()
            return carry

        lax.fori_loop(1, ROW, landed, 0)
        pick[p] = cand_in[p][gown[0]]

        def spread(k, carry):
            g_copy(p, k).start()
            return carry

        lax.fori_loop(1, ROW, spread, 0)
        for copy in self_copies(p):
            copy.start()

    for p in range(PAIRS):
        one_pair(p)

    for group in halos:
        for copy in group:
            copy.wait()

    def finish(p):
        for way in range(2):
            for t in range(8):
                for a in range(2):
                    if used(way, t, a):
                        z_copy(p, way, t, a).wait_send()
        for copy in self_copies(p):
            copy.wait()

        def ends(k, carry):
            c_copy(p, k).wait_send()
            x_copy(p, k).wait()
            g_copy(p, k).wait()
            return carry

        lax.fori_loop(1, ROW, ends, 0)

    for p in range(PAIRS):
        finish(p)


def exchange(kb, vb, req, gcode, gown):
    width = kb.shape[-1]
    block = (BLOCK, HEAD_DIM)
    dma = pltpu.SemaphoreType.DMA
    bf16 = jnp.bfloat16
    hbm = pl.BlockSpec(memory_space=pl.ANY)
    smem = pl.BlockSpec(memory_space=pltpu.SMEM)
    return pl.pallas_call(
        exchange_kernel,
        out_shape=(
            jax.ShapeDtypeStruct((PAIRS, ROW, CAP) + block, bf16),
            jax.ShapeDtypeStruct((PAIRS, ROW) + block, bf16),
            jax.ShapeDtypeStruct((2, SEQS, BLOCK, width), bf16),
            jax.ShapeDtypeStruct((2, SEQS, BLOCK, width), bf16),
        ),
        in_specs=[hbm, hbm, pl.BlockSpec(memory_space=pltpu.VMEM), smem, smem],
        out_specs=(hbm, hbm, hbm, hbm),
        scratch_shapes=[
            *([pltpu.VMEM((NZ * OWN,) + block, bf16)] * PAIRS),
            *([pltpu.VMEM((ROW,) + block, bf16)] * PAIRS),
            pltpu.VMEM((PAIRS, ROW, CAP) + block, bf16),
            pltpu.VMEM((PAIRS, ROW) + block, bf16),
            pltpu.VMEM((PAIRS,) + block, bf16),
            pltpu.VMEM((ROW, 8, 128), jnp.int32),
            pltpu.SMEM((ROW, 8, 128), jnp.int32),
            dma((PAIRS,)),
            dma((PAIRS, 32)), dma((PAIRS, 32)),
            dma((PAIRS, ROW)), dma((PAIRS, ROW)),
            dma((PAIRS, ROW)), dma((PAIRS, ROW)),
            dma((PAIRS, ROW)), dma((PAIRS, ROW)),
            dma((4 * SEQS,)), dma((4 * SEQS,)),
            dma((ROW,)), dma((ROW,)),
            dma((ROW,)), dma((1,)),
        ],
        compiler_params=pltpu.CompilerParams(
            collective_id=0, has_side_effects=True, vmem_limit_bytes=40 << 20
        ),
        name="exchange",
    )(kb, vb, req, gcode, gown)


def attend_kernel(slots, gslots, counts, q, kb, vb, hk, hv, g0, g1, *rest):
    rand, out = rest[: BPD * RMAX], rest[BPD * RMAX]
    s = pl.program_id(0)
    scale = HEAD_DIM ** (-0.5)
    width = (3 + GLOB + RMAX) * BLOCK
    column = lax.broadcasted_iota(jnp.int32, (BLOCK, width), 1)
    for j in range(BPD):
        live = column < (3 + GLOB) * BLOCK + counts[s * BPD + j] * BLOCK
        for h in range(2):
            lanes = slice(h * HEAD_DIM, (h + 1) * HEAD_DIM)

            def rows(own, halo, p):
                window = [halo[0, 0, :, lanes], own[0, :, lanes], own[1, :, lanes], halo[1, 0, :, lanes]]
                picked = [rand[j * RMAX + r][p, 0] for r in range(RMAX)]
                return jnp.concatenate(window[j : j + 3] + [g0[p, 0], g1[p, 0]] + picked, axis=0)

            keys = rows(kb, hk, 2 * h)
            values = rows(vb, hv, 2 * h + 1)
            scores = lax.dot_general(
                q[j, :, lanes], keys, (((1,), (1,)), ((), ())), preferred_element_type=jnp.float32
            ) * scale
            masked = jnp.where(live, scores, -1e30)
            peak = jnp.max(masked, axis=-1, keepdims=True)
            weights = jnp.where(live, jnp.exp(masked - peak), 0.0)
            total = jnp.sum(weights, axis=-1, keepdims=True)
            weighted = jnp.dot(
                weights.astype(jnp.bfloat16), values, preferred_element_type=jnp.float32
            )
            out[j, :, lanes] = (weighted / total).astype(jnp.bfloat16)


def attend(slots, gslots, counts, q, kb, vb, hk, hv, glob, rcv):
    width = q.shape[-1]
    pair = pl.BlockSpec((BPD, BLOCK, width), lambda s, *_: (s, 0, 0))
    halo = pl.BlockSpec((2, 1, BLOCK, width), lambda s, *_: (0, s, 0, 0))

    def shared(g):
        return pl.BlockSpec(
            (PAIRS, 1, BLOCK, HEAD_DIM), lambda s, sl, gs, ct: (0, gs[s * GLOB + g], 0, 0)
        )

    def random(n):
        return pl.BlockSpec(
            (PAIRS, 1, BLOCK, HEAD_DIM), lambda s, sl, gs, ct: (0, sl[s * BPD * RMAX + n], 0, 0)
        )

    return pl.pallas_call(
        attend_kernel,
        out_shape=jax.ShapeDtypeStruct(q.shape, q.dtype),
        grid_spec=pltpu.PrefetchScalarGridSpec(
            num_scalar_prefetch=3,
            grid=(SEQS,),
            in_specs=[pair, pair, pair, halo, halo, shared(0), shared(1)]
            + [random(n) for n in range(BPD * RMAX)],
            out_specs=pair,
        ),
        name="attend",
    )(slots, gslots, counts, q, kb, vb, hk, hv, glob, glob, *([rcv] * (BPD * RMAX)))


def on_device(queries, keys, values, out_weight, global_ids, rand_ids, rand_count):
    seq_count, seq_rows, width = queries.shape
    q = queries.reshape(OWN, BLOCK, width)
    kb = keys.reshape(OWN, BLOCK, width)
    vb = values.reshape(OWN, BLOCK, width)
    ctx = lax.axis_index("ctx")
    my_z = (ctx // NC) % NZ
    me = (ctx // (NZ * NC)) * NC + ctx % NC

    def place(ids, seq):
        owner = ids // BPD
        row = (owner // (NZ * NC)) * NC + owner % NC
        code = (((owner // NC) % NZ - my_z) % NZ) * OWN + seq * BPD + ids % BPD
        return row, code

    seq_of = jnp.arange(SEQS, dtype=jnp.int32)
    row, code = place(rand_ids, seq_of[:, None, None])
    live = (jnp.arange(RMAX, dtype=jnp.int32) < rand_count[:, :, None]).reshape(-1)
    turn = ((me - row) % ROW).reshape(-1)
    code = code.reshape(-1)
    number = jnp.arange(turn.shape[0], dtype=jnp.int32)
    same = (turn[:, None] == turn[None, :]) & live[None, :] & (number[None, :] < number[:, None])
    rank = jnp.sum(same.astype(jnp.int32), axis=1)
    slots = jnp.where(live, turn * CAP + rank, 0)
    place_of = jnp.arange(ROW, dtype=jnp.int32)[:, None] * CAP + jnp.minimum(
        jnp.arange(128, dtype=jnp.int32), CAP
    )
    valid = jnp.arange(128, dtype=jnp.int32) < CAP
    hit = (place_of[:, :, None] == slots[None, None, :]) & live & valid[None, :, None]
    req = jnp.sum(jnp.where(hit, code[None, None, :], 0), axis=2)
    req = jnp.broadcast_to(req[:, None, :], (ROW, 8, 128))

    grow, gcode = place(global_ids, seq_of[:, None])
    grow, gcode = grow.reshape(-1), gcode.reshape(-1)
    gown = ((me - grow) % ROW)[me].reshape(1)
    gslots = (me - jnp.arange(ROW, dtype=jnp.int32)) % ROW

    rcv, glob, halo_k, halo_v = exchange(kb, vb, req, gcode, gown)
    attention = attend(
        slots, gslots, rand_count.reshape(-1), q, kb, vb, halo_k, halo_v, glob,
        rcv.reshape(PAIRS, ROW * CAP, BLOCK, HEAD_DIM),
    ).reshape(seq_count, seq_rows, width)
    projected = jnp.einsum(
        "stf,fo->sto",
        lax.all_gather(attention, "head", axis=2, tiled=True),
        out_weight,
        preferred_element_type=jnp.float32,
    )
    return projected.astype(jnp.bfloat16)


def solution(mesh):
    placed = (
        P(None, "ctx", "head"),
        P(None, "ctx", "head"),
        P(None, "ctx", "head"),
        P(None, "head"),
        P(),
        P(None, "ctx", None),
        P(None, "ctx"),
    )
    return jax.shard_map(
        on_device, mesh=mesh, in_specs=placed, out_specs=P(None, "ctx", "head"), check_vma=False
    )
```

```python
import jax
import jax.numpy as jnp
from jax import lax
from jax.experimental import pallas as pl
from jax.experimental.pallas import tpu as pltpu
from jax.sharding import PartitionSpec as P

HEAD_DIM = 128
BLOCK = 64
GLOB = 2
RMAX = 4
NX, NZ, NC = 4, 16, 2
ROW = NX * NC
SEQS = 4
BPD = 2
OWN = SEQS * BPD
CAP = 16
PAIRS = 4
SPLIT = 4
PART = OWN // SPLIT
MESH = pl.DeviceIdType.MESH


GROUPS = ((0, 5), (5, 9), (9, 13), (13, 16))
NY = 4


def slot_of(d):
    return 0 if d == 0 else (2 * d - 1 if d < 8 else (15 if d == 8 else 2 * (NZ - d)))


ORDER = sorted(range(NZ), key=slot_of)


def exchange_kernel(
    kb, vb, req, gdist, gsel, gown, rcv, glob, halo_k, halo_v, *scratch
):
    gath = [scratch[p * NZ : (p + 1) * NZ] for p in range(PAIRS)]
    cand_in = scratch[PAIRS * NZ : PAIRS * (NZ + 1)]
    (
        pack, cand, pick, req_in, req_s,
        own_sem, z_send, z_recv, x_send, x_recv, c_send, c_recv, g_send, g_recv,
        h_send, h_recv, r_send, r_recv, s_sem,
    ) = scratch[PAIRS * (NZ + 1) :]
    ctx = lax.axis_index("ctx")
    head = lax.axis_index("head")
    x, z, c = ctx // (NZ * NC), (ctx // NC) % NZ, ctx % NC
    me = x * NC + c

    def at_z(step):
        return (x * (NZ * NC) + ((z + step + NZ) % NZ) * NC + c, head)

    def at_row(r):
        return ((r // NC) * (NZ * NC) + z * NC + r % NC, head)

    count = NX * NZ * NC
    right = ((ctx + 1) % count, head)
    left = ((ctx + count - 1) % count, head)

    own = [
        pltpu.make_async_copy(
            (kb, vb)[p % 2].at[:, :, pl.ds((p // 2) * HEAD_DIM, HEAD_DIM)],
            gath[p][0],
            own_sem.at[p],
        )
        for p in range(PAIRS)
    ]
    for copy in own:
        copy.start()
    own_req = pltpu.make_async_copy(req.at[0], req_s.at[0], s_sem.at[0])
    own_req.start()

    barrier = pltpu.get_barrier_semaphore()
    peers = [at_z(1), at_z(-1), right, left] + [at_row((me + k) % ROW) for k in range(1, ROW)]
    for peer in peers:
        pl.semaphore_signal(barrier, inc=1, device_id=peer, device_id_type=MESH)
    pl.semaphore_wait(barrier, len(peers))

    def req_copy(k):
        return pltpu.make_async_remote_copy(
            src_ref=req.at[k], dst_ref=req_in.at[k],
            send_sem=r_send.at[k], recv_sem=r_recv.at[k],
            device_id=at_row((me + ROW - k) % ROW), device_id_type=MESH,
        )

    for k in range(1, ROW):
        req_copy(k).start()

    def z_copy(p, way, t, a):
        if way == 0:
            src, dst, peer = (-t) % NZ, (-t - 1) % NZ, at_z(1)
        else:
            src, dst, peer = t, t + 1, at_z(-1)
        part = pl.ds(a * PART, PART)
        return pltpu.make_async_remote_copy(
            src_ref=gath[p][src].at[part],
            dst_ref=gath[p][dst].at[part],
            send_sem=z_send.at[p, (way * 8 + t) * SPLIT + a],
            recv_sem=z_recv.at[p, (way * 8 + t) * SPLIT + a],
            device_id=peer, device_id_type=MESH,
        )

    def used(way, t, a):
        return t < 7 or a // (SPLIT // 2) == way

    for copy in own:
        copy.wait()
    for a in range(SPLIT):
        for way in range(2):
            z_copy(0, way, 0, a).start()

    halos = []
    for i, (src, dst) in enumerate(((kb, halo_k), (vb, halo_v))):
        for side in range(2):
            for s in range(SEQS):
                halos.append(
                    pltpu.make_async_remote_copy(
                        src_ref=src.at[2 * s + 1 - side], dst_ref=dst.at[side, s],
                        send_sem=h_send.at[(i * 2 + side) * SEQS + s],
                        recv_sem=h_recv.at[(i * 2 + side) * SEQS + s],
                        device_id=(right, left)[side], device_id_type=MESH,
                    )
                )
    for copy in halos:
        copy.start()

    own_req.wait()
    for k in range(1, ROW):
        req_copy(k).wait()
    rest = [
        pltpu.make_async_copy(req_in.at[k], req_s.at[k], s_sem.at[k]) for k in range(1, ROW)
    ]
    for copy in rest:
        copy.start()
    for copy in rest:
        copy.wait()

    def x_copy(p, g, k):
        low, high = GROUPS[g]
        return pltpu.make_async_remote_copy(
            src_ref=pack.at[p, k, pl.ds(low, high - low)],
            dst_ref=rcv.at[p, k, pl.ds(low, high - low)],
            send_sem=x_send.at[p * len(GROUPS) + g, k],
            recv_sem=x_recv.at[p * len(GROUPS) + g, k],
            device_id=at_row((me + k) % ROW), device_id_type=MESH,
        )

    def c_copy(p, k):
        return pltpu.make_async_remote_copy(
            src_ref=cand.at[p, (me + k) % ROW], dst_ref=cand_in[p].at[k],
            send_sem=c_send.at[p, k], recv_sem=c_recv.at[p, k],
            device_id=at_row((me + k) % ROW), device_id_type=MESH,
        )

    def g_copy(p, k):
        return pltpu.make_async_remote_copy(
            src_ref=pick.at[p], dst_ref=glob.at[p, k],
            send_sem=g_send.at[p, k], recv_sem=g_recv.at[p, k],
            device_id=at_row((me + k) % ROW), device_id_type=MESH,
        )

    def push(p, g):
        low, high = GROUPS[g]
        for n in range(low, high):
            rcv[p, 0, n] = gath[p][ORDER[n]][req_s[0, 0, n]]

        def fill(k, carry):
            for n in range(low, high):
                pack[p, k, n] = gath[p][ORDER[n]][req_s[k, 0, n]]
            x_copy(p, g, k).start()
            return carry

        lax.fori_loop(1, ROW, fill, 0)

    def consider(p, dists):
        def one(q, carry):
            best = cand[p, q]
            for d in dists:
                best = lax.select(gdist[q] == d, gath[p][d][gsel[q]], best)
            cand[p, q] = best
            return carry

        lax.fori_loop(0, ROW, one, 0)

    def spread(p):
        def landed(k, carry):
            c_copy(p, k).wait_recv()
            return carry

        lax.fori_loop(1, ROW, landed, 0)
        chosen = cand_in[p][gown[0]]
        pick[p] = chosen
        glob[p, 0] = chosen

        def send(k, carry):
            g_copy(p, k).start()
            return carry

        lax.fori_loop(1, ROW, send, 0)

    def one_pair(p):
        def first(q, carry):
            cand[p, q] = gath[p][0][gsel[q]]
            return carry

        lax.fori_loop(0, ROW, first, 0)
        for t in range(1, 8):
            for a in range(SPLIT):
                for way in range(2):
                    z_copy(p, way, t - 1, a).wait_recv()
                    if used(way, t, a):
                        z_copy(p, way, t, a).start()
                    if t == 7 and p < PAIRS - 1:
                        z_copy(p + 1, way, 0, a).start()
            consider(p, (t, NZ - t))
            if t % 2 == 0:
                push(p, t // 2 - 1)
            if t == 3 and p > 0:
                spread(p - 1)
        for a in range(SPLIT):
            z_copy(p, a // (SPLIT // 2), 7, a).wait_recv()
        consider(p, (8,))

        def offer(k, carry):
            c_copy(p, k).start()
            return carry

        lax.fori_loop(1, ROW, offer, 0)
        push(p, 3)
        cand_in[p][0] = cand[p, me]

    for p in range(PAIRS):
        one_pair(p)
    spread(PAIRS - 1)

    for copy in halos:
        copy.wait()
    for p in range(PAIRS):
        for way in range(2):
            for t in range(8):
                for a in range(SPLIT):
                    if used(way, t, a):
                        z_copy(p, way, t, a).wait_send()

        def ends(k, carry, p=p):
            c_copy(p, k).wait_send()
            g_copy(p, k).wait()
            for g in range(len(GROUPS)):
                x_copy(p, g, k).wait()
            return carry

        lax.fori_loop(1, ROW, ends, 0)


def exchange(kb, vb, req, gdist, gsel, gown):
    width = kb.shape[-1]
    block = (BLOCK, HEAD_DIM)
    dma = pltpu.SemaphoreType.DMA
    bf16 = jnp.bfloat16
    hbm = pl.BlockSpec(memory_space=pl.ANY)
    vmem = pl.BlockSpec(memory_space=pltpu.VMEM)
    smem = pl.BlockSpec(memory_space=pltpu.SMEM)
    return pl.pallas_call(
        exchange_kernel,
        out_shape=(
            jax.ShapeDtypeStruct((PAIRS, ROW, CAP) + block, bf16),
            jax.ShapeDtypeStruct((PAIRS, ROW) + block, bf16),
            jax.ShapeDtypeStruct((2, SEQS, BLOCK, width), bf16),
            jax.ShapeDtypeStruct((2, SEQS, BLOCK, width), bf16),
        ),
        in_specs=[hbm, hbm, vmem, smem, smem, smem],
        out_specs=(vmem, vmem, vmem, vmem),
        scratch_shapes=[
            *([pltpu.VMEM((OWN,) + block, bf16)] * (PAIRS * NZ)),
            *([pltpu.VMEM((ROW,) + block, bf16)] * PAIRS),
            pltpu.VMEM((PAIRS, ROW, CAP) + block, bf16),
            pltpu.VMEM((PAIRS, ROW) + block, bf16),
            pltpu.VMEM((PAIRS,) + block, bf16),
            pltpu.VMEM((ROW, 8, 128), jnp.int32),
            pltpu.SMEM((ROW, 8, 128), jnp.int32),
            dma((PAIRS,)),
            dma((PAIRS, 16 * SPLIT)), dma((PAIRS, 16 * SPLIT)),
            dma((PAIRS * len(GROUPS), ROW)), dma((PAIRS * len(GROUPS), ROW)),
            dma((PAIRS, ROW)), dma((PAIRS, ROW)),
            dma((PAIRS, ROW)), dma((PAIRS, ROW)),
            dma((4 * SEQS,)), dma((4 * SEQS,)),
            dma((ROW,)), dma((ROW,)),
            dma((ROW,)),
        ],
        compiler_params=pltpu.CompilerParams(
            collective_id=0, has_side_effects=True, vmem_limit_bytes=44 << 20
        ),
        name="exchange",
    )(kb, vb, req, gdist, gsel, gown)


def attend_kernel(slots, gslots, counts, q, kb, vb, hk, hv, glob, rcv, w, out, att, att_in, send, recv):
    ctx = lax.axis_index("ctx")
    y = lax.axis_index("head")
    barrier = pltpu.get_barrier_semaphore()
    for k in range(1, NY):
        pl.semaphore_signal(
            barrier, inc=1, device_id=(ctx, (y + k) % NY), device_id_type=MESH
        )

    scale = HEAD_DIM ** (-0.5)
    width = (3 + GLOB + RMAX) * BLOCK
    column = lax.broadcasted_iota(jnp.int32, (BLOCK, width), 1)

    def y_copy(k, h):
        lanes = pl.ds(h * HEAD_DIM, HEAD_DIM)
        return pltpu.make_async_remote_copy(
            src_ref=att.at[:, lanes], dst_ref=att_in.at[k - 1, :, lanes],
            send_sem=send.at[k, h], recv_sem=recv.at[k, h],
            device_id=(ctx, (y + k) % NY), device_id_type=MESH,
        )

    for h in range(2):
        lanes = slice(h * HEAD_DIM, (h + 1) * HEAD_DIM)

        def one_seq(s, carry, h=h, lanes=lanes):
            def rows(own, halo, p, j):
                window = [
                    halo[0, s, :, lanes], own[2 * s, :, lanes],
                    own[2 * s + 1, :, lanes], halo[1, s, :, lanes],
                ]
                shared = [glob[p, gslots[s * GLOB + g]] for g in range(GLOB)]
                picked = [rcv[p, slots[(s * BPD + j) * RMAX + r]] for r in range(RMAX)]
                return jnp.concatenate(window[j : j + 3] + shared + picked, axis=0)

            for j in range(BPD):
                live = column < (3 + GLOB) * BLOCK + counts[s * BPD + j] * BLOCK
                scores = lax.dot_general(
                    q[2 * s + j, :, lanes], rows(kb, hk, 2 * h, j), (((1,), (1,)), ((), ())),
                    preferred_element_type=jnp.float32,
                ) * scale
                masked = jnp.where(live, scores, -1e30)
                peak = jnp.max(masked, axis=-1, keepdims=True)
                weights = jnp.where(live, jnp.exp(masked - peak), 0.0)
                total = jnp.sum(weights, axis=-1, keepdims=True)
                weighted = jnp.dot(
                    weights.astype(jnp.bfloat16), rows(vb, hv, 2 * h + 1, j),
                    preferred_element_type=jnp.float32,
                )
                at = pl.ds(pl.multiple_of((2 * s + j) * BLOCK, BLOCK), BLOCK)
                att[at, lanes] = (weighted / total).astype(jnp.bfloat16)
            return carry

        lax.fori_loop(0, SEQS, one_seq, 0)
        if h == 0:
            pl.semaphore_wait(barrier, NY - 1)
        for k in range(1, NY):
            y_copy(k, h).start()

    def rows_of(k):
        return w[pl.ds(pl.multiple_of(((y + NY - k) % NY) * 256, 256), 256), :]

    for k in range(1, NY):
        for h in range(2):
            y_copy(k, h).wait_recv()

    def project(i, carry):
        at = pl.ds(pl.multiple_of(i * 128, 128), 128)
        total = jnp.dot(att[at, :], rows_of(0), preferred_element_type=jnp.float32)
        for k in range(1, NY):
            total += jnp.dot(att_in[k - 1, at, :], rows_of(k), preferred_element_type=jnp.float32)
        out[at, :] = total.astype(jnp.bfloat16)
        return carry

    lax.fori_loop(0, 4, project, 0)
    for k in range(1, NY):
        for h in range(2):
            y_copy(k, h).wait_send()


def attend(slots, gslots, counts, q, kb, vb, hk, hv, glob, rcv, w):
    rows = OWN * BLOCK
    width = q.shape[-1]
    vmem = pl.BlockSpec(memory_space=pltpu.VMEM)
    smem = pl.BlockSpec(memory_space=pltpu.SMEM)
    dma = pltpu.SemaphoreType.DMA
    return pl.pallas_call(
        attend_kernel,
        out_shape=jax.ShapeDtypeStruct((rows, w.shape[1]), q.dtype),
        in_specs=[smem] * 3 + [vmem] * 8,
        out_specs=vmem,
        scratch_shapes=[
            pltpu.VMEM((rows, width), jnp.bfloat16),
            pltpu.VMEM((NY - 1, rows, width), jnp.bfloat16),
            dma((NY, 2)), dma((NY, 2)),
        ],
        compiler_params=pltpu.CompilerParams(
            collective_id=1, has_side_effects=True, vmem_limit_bytes=30 << 20
        ),
        name="attend",
    )(slots, gslots, counts, q, kb, vb, hk, hv, glob, rcv, w)


def on_device(queries, keys, values, out_weight, global_ids, rand_ids, rand_count):
    seq_count, seq_rows, width = queries.shape
    q = queries.reshape(OWN, BLOCK, width)
    kb = keys.reshape(OWN, BLOCK, width)
    vb = values.reshape(OWN, BLOCK, width)
    ctx = lax.axis_index("ctx")
    my_z = (ctx // NC) % NZ
    me = (ctx // (NZ * NC)) * NC + ctx % NC

    def place(ids, seq):
        owner = ids // BPD
        row = (owner // (NZ * NC)) * NC + owner % NC
        dist = ((owner // NC) % NZ - my_z) % NZ
        return row, dist, seq * BPD + ids % BPD

    seq_of = jnp.arange(SEQS, dtype=jnp.int32)
    row, dist, choice = place(rand_ids, seq_of[:, None, None])
    live = (jnp.arange(RMAX, dtype=jnp.int32) < rand_count[:, :, None]).reshape(-1)
    where = jnp.where(dist < 8, jnp.maximum(2 * dist - 1, 0), 2 * (NZ - dist))
    where = jnp.where(dist == 8, CAP - 1, where)
    slots = jnp.where(live, (((me - row) % ROW) * CAP + where).reshape(-1), 0)
    lane = jnp.arange(128, dtype=jnp.int32)
    place_of = jnp.arange(ROW, dtype=jnp.int32)[:, None] * CAP + lane
    hit = (place_of[:, :, None] == slots) & live & (lane < CAP)[None, :, None]
    req = jnp.max(jnp.where(hit, choice.reshape(-1), 0), axis=2)
    req = jnp.broadcast_to(req[:, None, :], (ROW, 8, 128))

    grow, gdist, gsel = place(global_ids, seq_of[:, None])
    gown = ((me - grow.reshape(-1)) % ROW)[me].reshape(1)
    gslots = (me - jnp.arange(ROW, dtype=jnp.int32)) % ROW

    rcv, glob, halo_k, halo_v = exchange(kb, vb, req, gdist.reshape(-1), gsel.reshape(-1), gown)
    return attend(
        slots, gslots, rand_count.reshape(-1), q, kb, vb, halo_k, halo_v, glob,
        rcv.reshape(PAIRS, ROW * CAP, BLOCK, HEAD_DIM), out_weight,
    ).reshape(seq_count, seq_rows, out_weight.shape[1])


def solution(mesh):
    placed = (
        P(None, "ctx", "head"),
        P(None, "ctx", "head"),
        P(None, "ctx", "head"),
        P(None, "head"),
        P(),
        P(None, "ctx", None),
        P(None, "ctx"),
    )
    return jax.shard_map(
        on_device, mesh=mesh, in_specs=placed, out_specs=P(None, "ctx", "head"), check_vma=False
    )
```

```python
import jax
import jax.numpy as jnp
from jax import lax
from jax.experimental import pallas as pl
from jax.experimental.pallas import tpu as pltpu
from jax.sharding import PartitionSpec as P

HEAD_DIM = 128
BLOCK = 64
GLOB = 2
RMAX = 4
NX, NZ, NC = 4, 16, 2
ROW = NX * NC
SEQS = 4
BPD = 2
OWN = SEQS * BPD
CAP = 16
PAIRS = 4
SPLIT = 4
PART = OWN // SPLIT
MESH = pl.DeviceIdType.MESH


GROUPS = ((0, 1), (1, 5), (5, 9), (9, 13), (13, 16))
ROWS = OWN * BLOCK
KEYS = (3 + GLOB + RMAX) * BLOCK
NY = 4
STEPS = ((5, 2), (6, 0), (6, 2), (7, 0))


def slot_of(d):
    return 0 if d == 0 else (2 * d - 1 if d < 8 else (15 if d == 8 else 2 * (NZ - d)))


ORDER = sorted(range(NZ), key=slot_of)


def exchange_kernel(
    q_any, k8, v8, k4, v4, w_any, req, gdist, gsel, gown, slots, counts, out, *scratch
):
    gath = [scratch[p * NZ : (p + 1) * NZ] for p in range(PAIRS)]
    rest = scratch[PAIRS * NZ :]
    cand_in, rcv, glob, win = (rest[i * PAIRS : (i + 1) * PAIRS] for i in range(4))
    (
        pack, cand, pick, req_in, req_s, q, w, weights, totals, att, att_in, partial,
        own_sem, z_send, z_recv, x_send, x_recv, c_send, c_recv, g_send, g_recv,
        h_send, h_recv, r_send, r_recv, s_sem, y_send, y_recv,
    ) = rest[4 * PAIRS :]
    ctx = lax.axis_index("ctx")
    head = lax.axis_index("head")
    x, z, c = ctx // (NZ * NC), (ctx // NC) % NZ, ctx % NC
    me = x * NC + c

    def at_z(step):
        return (x * (NZ * NC) + ((z + step + NZ) % NZ) * NC + c, head)

    def at_row(r):
        return ((r // NC) * (NZ * NC) + z * NC + r % NC, head)

    count = NX * NZ * NC
    right = ((ctx + 1) % count, head)
    left = ((ctx + count - 1) % count, head)

    own = [
        pltpu.make_async_copy(
            (k8, v8)[p % 2].at[:, :, pl.ds((p // 2) * HEAD_DIM, HEAD_DIM)],
            gath[p][0],
            own_sem.at[p],
        )
        for p in range(PAIRS)
    ]
    late = [
        pltpu.make_async_copy(
            (k4, v4)[p % 2].at[:, :, :, pl.ds((p // 2) * HEAD_DIM, HEAD_DIM)],
            win[p].at[:, pl.ds(1, BPD)],
            own_sem.at[PAIRS + p],
        )
        for p in range(PAIRS)
    ] + [
        pltpu.make_async_copy(q_any, q, own_sem.at[2 * PAIRS]),
        pltpu.make_async_copy(w_any, w, own_sem.at[2 * PAIRS + 1]),
    ]
    for copy in own:
        copy.start()
    own_req = pltpu.make_async_copy(req.at[0], req_s.at[0], s_sem.at[0])
    own_req.start()
    for copy in late:
        copy.start()

    barrier = pltpu.get_barrier_semaphore()
    peers = [at_z(1), at_z(-1), right, left] + [at_row((me + k) % ROW) for k in range(1, ROW)]
    peers += [(ctx, (head + k) % NY) for k in range(1, NY)]
    for peer in peers:
        pl.semaphore_signal(barrier, inc=1, device_id=peer, device_id_type=MESH)
    pl.semaphore_wait(barrier, len(peers))

    def req_copy(k):
        return pltpu.make_async_remote_copy(
            src_ref=req.at[k], dst_ref=req_in.at[k],
            send_sem=r_send.at[k], recv_sem=r_recv.at[k],
            device_id=at_row((me + ROW - k) % ROW), device_id_type=MESH,
        )

    for k in range(1, ROW):
        req_copy(k).start()

    def z_copy(p, way, t, a):
        if way == 0:
            src, dst, peer = (-t) % NZ, (-t - 1) % NZ, at_z(1)
        else:
            src, dst, peer = t, t + 1, at_z(-1)
        part = pl.ds(a * PART, PART)
        return pltpu.make_async_remote_copy(
            src_ref=gath[p][src].at[part],
            dst_ref=gath[p][dst].at[part],
            send_sem=z_send.at[p, (way * 8 + t) * SPLIT + a],
            recv_sem=z_recv.at[p, (way * 8 + t) * SPLIT + a],
            device_id=peer, device_id_type=MESH,
        )

    def used(way, t, a):
        return t < 7 or a // (SPLIT // 2) == way

    for copy in own:
        copy.wait()
    for a in range(SPLIT):
        for way in range(2):
            z_copy(0, way, 0, a).start()

    halos = [
        pltpu.make_async_remote_copy(
            src_ref=(k4, v4)[p % 2].at[:, 1 - side, :, pl.ds((p // 2) * HEAD_DIM, HEAD_DIM)],
            dst_ref=win[p].at[:, 3 * side],
            send_sem=h_send.at[2 * p + side],
            recv_sem=h_recv.at[2 * p + side],
            device_id=(right, left)[side], device_id_type=MESH,
        )
        for p in range(PAIRS)
        for side in range(2)
    ]
    for copy in halos:
        copy.start()

    own_req.wait()
    for k in range(1, ROW):
        req_copy(k).wait()
    lists = [
        pltpu.make_async_copy(req_in.at[k], req_s.at[k], s_sem.at[k]) for k in range(1, ROW)
    ]
    for copy in lists:
        copy.start()
    for copy in lists:
        copy.wait()

    def x_copy(p, g, k):
        low, high = GROUPS[g]
        return pltpu.make_async_remote_copy(
            src_ref=pack.at[p, k, pl.ds(low, high - low)],
            dst_ref=rcv[p].at[pl.ds(k * CAP + low, high - low)],
            send_sem=x_send.at[p * len(GROUPS) + g, k],
            recv_sem=x_recv.at[p * len(GROUPS) + g, k],
            device_id=at_row((me + k) % ROW), device_id_type=MESH,
        )

    def c_copy(p, k):
        return pltpu.make_async_remote_copy(
            src_ref=cand.at[p, (me + k) % ROW], dst_ref=cand_in[p].at[k],
            send_sem=c_send.at[p, k], recv_sem=c_recv.at[p, k],
            device_id=at_row((me + k) % ROW), device_id_type=MESH,
        )

    def g_copy(p, k):
        return pltpu.make_async_remote_copy(
            src_ref=pick.at[p], dst_ref=glob[p].at[k],
            send_sem=g_send.at[p, k], recv_sem=g_recv.at[p, k],
            device_id=at_row((me + k) % ROW), device_id_type=MESH,
        )

    def push(p, g):
        low, high = GROUPS[g]
        for n in range(low, high):
            rcv[p][n] = gath[p][ORDER[n]][req_s[0, 0, n]]

        def fill(k, carry):
            for n in range(low, high):
                pack[p, k, n] = gath[p][ORDER[n]][req_s[k, 0, n]]
            x_copy(p, g, k).start()
            return carry

        lax.fori_loop(1, ROW, fill, 0)

    def consider(p, dists):
        def one(q, carry):
            best = cand[p, q]
            for d in dists:
                best = lax.select(gdist[q] == d, gath[p][d][gsel[q]], best)
            cand[p, q] = best
            return carry

        lax.fori_loop(0, ROW, one, 0)

    def spread(p):
        def landed(k, carry):
            c_copy(p, k).wait_recv()
            return carry

        lax.fori_loop(1, ROW, landed, 0)
        chosen = cand_in[p][gown[0]]
        pick[p] = chosen
        glob[p][0] = chosen

        def send(k, carry):
            g_copy(p, k).start()
            return carry

        lax.fori_loop(1, ROW, send, 0)

    def settle(p):
        def landed(k, carry):
            g_copy(p, k).wait_recv()
            for g in range(len(GROUPS)):
                x_copy(p, g, k).wait_recv()
            return carry

        lax.fori_loop(1, ROW, landed, 0)
        for side in range(2):
            halos[2 * p + side].wait_recv()

    def rows(p, n):
        s, j = n // BPD, n % BPD
        window = [win[p][s, j + i] for i in range(3)]
        shared = [glob[p][(me + ROW - (s * GLOB + g)) % ROW] for g in range(GLOB)]
        picked = [rcv[p][slots[n * RMAX + r]] for r in range(RMAX)]
        return jnp.concatenate(window + shared + picked, axis=0)

    column = lax.broadcasted_iota(jnp.int32, (BLOCK, KEYS), 1)

    def score(h, low, high):
        def one(n, carry):
            live = column < (3 + GLOB) * BLOCK + counts[n] * BLOCK
            scores = lax.dot_general(
                q[n, :, h * HEAD_DIM : (h + 1) * HEAD_DIM], rows(2 * h, n),
                (((1,), (1,)), ((), ())), preferred_element_type=jnp.float32,
            ) * (HEAD_DIM ** (-0.5))
            masked = jnp.where(live, scores, -1e30)
            peak = jnp.max(masked, axis=-1, keepdims=True)
            grown = jnp.where(live, jnp.exp(masked - peak), 0.0)
            weights[n] = grown.astype(jnp.bfloat16)
            totals[n] = jnp.broadcast_to(
                jnp.sum(grown, axis=-1, keepdims=True), (BLOCK, HEAD_DIM)
            )
            return carry

        lax.fori_loop(low, high, one, 0)

    def mix(h, low, high):
        def one(n, carry):
            weighted = jnp.dot(
                weights[n], rows(2 * h + 1, n), preferred_element_type=jnp.float32
            )
            at = pl.ds(pl.multiple_of(n * BLOCK, BLOCK), BLOCK)
            att[h, at, :] = (weighted / totals[n]).astype(jnp.bfloat16)
            return carry

        lax.fori_loop(low, high, one, 0)

    def y_copy(k, h, part):
        at = pl.ds(part * (ROWS // 2), ROWS // 2)
        return pltpu.make_async_remote_copy(
            src_ref=att.at[h, at], dst_ref=att_in.at[k - 1, h, at],
            send_sem=y_send.at[k, 2 * h + part], recv_sem=y_recv.at[k, 2 * h + part],
            device_id=(ctx, (head + k) % NY), device_id_type=MESH,
        )

    def share(h, part):
        for k in range(1, NY):
            y_copy(k, h, part).start()

    def compute(p, step):
        h, quarter = p // 2, (2 * step, 2 * step + 2)
        if step == 0:
            settle(p)
        (mix if p % 2 else score)(h, *quarter)
        if p % 2 and step % 2:
            share(h, step // 2)

    def one_pair(p):
        def first(n, carry):
            cand[p, n] = gath[p][0][gsel[n]]
            return carry

        lax.fori_loop(0, ROW, first, 0)
        for t in range(1, 8):
            for a in range(SPLIT):
                for way in range(2):
                    z_copy(p, way, t - 1, a).wait_recv()
                    if used(way, t, a):
                        z_copy(p, way, t, a).start()
                    if t == 7 and p < PAIRS - 1:
                        z_copy(p + 1, way, 0, a).start()
                if p > 0 and (t, a) in STEPS:
                    compute(p - 1, STEPS.index((t, a)))
            consider(p, (t, NZ - t))
            if t % 2 == 0:
                push(p, t // 2)
            if t == 3 and p > 0:
                spread(p - 1)
        for a in range(SPLIT):
            z_copy(p, a // (SPLIT // 2), 7, a).wait_recv()
        consider(p, (8,))

        def offer(k, carry):
            c_copy(p, k).start()
            return carry

        lax.fori_loop(1, ROW, offer, 0)
        push(p, 4)
        cand_in[p][0] = cand[p, me]

    for p in range(PAIRS):
        push(p, 0)
    for copy in late:
        copy.wait()
    for p in range(PAIRS):
        one_pair(p)
    spread(PAIRS - 1)
    for step in range(4):
        compute(PAIRS - 1, step)

    def feature_rows(k, h):
        start = ((head + NY - k) % NY) * (2 * HEAD_DIM) + h * HEAD_DIM
        return w[pl.ds(pl.multiple_of(start, HEAD_DIM), HEAD_DIM), :]

    for k in range(1, NY):
        for part in range(2):
            y_copy(k, 0, part).wait_recv()

    def project_first(i, carry):
        at = pl.ds(pl.multiple_of(i * 128, 128), 128)
        total = jnp.dot(att[0, at, :], feature_rows(0, 0), preferred_element_type=jnp.float32)
        total += jnp.dot(att[1, at, :], feature_rows(0, 1), preferred_element_type=jnp.float32)
        for k in range(1, NY):
            total += jnp.dot(
                att_in[k - 1, 0, at, :], feature_rows(k, 0), preferred_element_type=jnp.float32
            )
        partial[at, :] = total
        return carry

    lax.fori_loop(0, ROWS // 128, project_first, 0)
    for k in range(1, NY):
        for part in range(2):
            y_copy(k, 1, part).wait_recv()

    def project_last(i, carry):
        at = pl.ds(pl.multiple_of(i * 128, 128), 128)
        total = partial[at, :]
        for k in range(1, NY):
            total += jnp.dot(
                att_in[k - 1, 1, at, :], feature_rows(k, 1), preferred_element_type=jnp.float32
            )
        out[at, :] = total.astype(jnp.bfloat16)
        return carry

    lax.fori_loop(0, ROWS // 128, project_last, 0)

    for copy in halos:
        copy.wait_send()
    for k in range(1, NY):
        for h in range(2):
            for part in range(2):
                y_copy(k, h, part).wait_send()
    for p in range(PAIRS):
        for way in range(2):
            for t in range(8):
                for a in range(SPLIT):
                    if used(way, t, a):
                        z_copy(p, way, t, a).wait_send()

        def ends(k, carry, p=p):
            c_copy(p, k).wait_send()
            g_copy(p, k).wait_send()
            for g in range(len(GROUPS)):
                x_copy(p, g, k).wait_send()
            return carry

        lax.fori_loop(1, ROW, ends, 0)


def exchange(q, keys, values, w, req, gdist, gsel, gown, slots, counts):
    width = q.shape[-1]
    block = (BLOCK, HEAD_DIM)
    dma = pltpu.SemaphoreType.DMA
    bf16 = jnp.bfloat16
    hbm = pl.BlockSpec(memory_space=pl.ANY)
    vmem = pl.BlockSpec(memory_space=pltpu.VMEM)
    smem = pl.BlockSpec(memory_space=pltpu.SMEM)
    k8, v8 = (kv.reshape(OWN, BLOCK, width) for kv in (keys, values))
    k4, v4 = (kv.reshape(SEQS, BPD, BLOCK, width) for kv in (keys, values))
    return pl.pallas_call(
        exchange_kernel,
        out_shape=jax.ShapeDtypeStruct((ROWS, w.shape[1]), bf16),
        in_specs=[hbm] * 6 + [vmem] + [smem] * 5,
        out_specs=vmem,
        scratch_shapes=[
            *([pltpu.VMEM((OWN,) + block, bf16)] * (PAIRS * NZ)),
            *([pltpu.VMEM((ROW,) + block, bf16)] * PAIRS),
            *([pltpu.VMEM((ROW * CAP,) + block, bf16)] * PAIRS),
            *([pltpu.VMEM((ROW,) + block, bf16)] * PAIRS),
            *([pltpu.VMEM((SEQS, BPD + 2) + block, bf16)] * PAIRS),
            pltpu.VMEM((PAIRS, ROW, CAP) + block, bf16),
            pltpu.VMEM((PAIRS, ROW) + block, bf16),
            pltpu.VMEM((PAIRS,) + block, bf16),
            pltpu.VMEM((ROW, 8, 128), jnp.int32),
            pltpu.SMEM((ROW, 8, 128), jnp.int32),
            pltpu.VMEM((OWN, BLOCK, width), bf16),
            pltpu.VMEM(w.shape, bf16),
            pltpu.VMEM((OWN, BLOCK, KEYS), bf16),
            pltpu.VMEM((OWN,) + block, jnp.float32),
            pltpu.VMEM((2, ROWS, HEAD_DIM), bf16),
            pltpu.VMEM((NY - 1, 2, ROWS, HEAD_DIM), bf16),
            pltpu.VMEM((ROWS, w.shape[1]), jnp.float32),
            dma((2 * PAIRS + 2,)),
            dma((PAIRS, 16 * SPLIT)), dma((PAIRS, 16 * SPLIT)),
            dma((PAIRS * len(GROUPS), ROW)), dma((PAIRS * len(GROUPS), ROW)),
            dma((PAIRS, ROW)), dma((PAIRS, ROW)),
            dma((PAIRS, ROW)), dma((PAIRS, ROW)),
            dma((2 * PAIRS,)), dma((2 * PAIRS,)),
            dma((ROW,)), dma((ROW,)),
            dma((ROW,)),
            dma((NY, 4)), dma((NY, 4)),
        ],
        compiler_params=pltpu.CompilerParams(
            collective_id=0, has_side_effects=True, vmem_limit_bytes=52 << 20
        ),
        name="exchange",
    )(q, k8, v8, k4, v4, w, req, gdist, gsel, gown, slots, counts)


def on_device(queries, keys, values, out_weight, global_ids, rand_ids, rand_count):
    seq_count, seq_rows, width = queries.shape
    q = queries.reshape(OWN, BLOCK, width)
    ctx = lax.axis_index("ctx")
    my_z = (ctx // NC) % NZ
    me = (ctx // (NZ * NC)) * NC + ctx % NC

    def place(ids, seq):
        owner = ids // BPD
        row = (owner // (NZ * NC)) * NC + owner % NC
        dist = ((owner // NC) % NZ - my_z) % NZ
        return row, dist, seq * BPD + ids % BPD

    seq_of = jnp.arange(SEQS, dtype=jnp.int32)
    row, dist, choice = place(rand_ids, seq_of[:, None, None])
    live = (jnp.arange(RMAX, dtype=jnp.int32) < rand_count[:, :, None]).reshape(-1)
    where = jnp.where(dist < 8, jnp.maximum(2 * dist - 1, 0), 2 * (NZ - dist))
    where = jnp.where(dist == 8, CAP - 1, where)
    slots = jnp.where(live, (((me - row) % ROW) * CAP + where).reshape(-1), 0)
    lane = jnp.arange(128, dtype=jnp.int32)
    place_of = jnp.arange(ROW, dtype=jnp.int32)[:, None] * CAP + lane
    hit = (place_of[:, :, None] == slots) & live & (lane < CAP)[None, :, None]
    req = jnp.max(jnp.where(hit, choice.reshape(-1), 0), axis=2)
    req = jnp.broadcast_to(req[:, None, :], (ROW, 8, 128))

    grow, gdist, gsel = place(global_ids, seq_of[:, None])
    gown = ((me - grow.reshape(-1)) % ROW)[me].reshape(1)

    return exchange(
        q, keys, values, out_weight, req, gdist.reshape(-1), gsel.reshape(-1), gown,
        slots, rand_count.reshape(-1),
    ).reshape(seq_count, seq_rows, out_weight.shape[1])


def solution(mesh):
    placed = (
        P(None, "ctx", "head"),
        P(None, "ctx", "head"),
        P(None, "ctx", "head"),
        P(None, "head"),
        P(),
        P(None, "ctx", None),
        P(None, "ctx"),
    )
    return jax.shard_map(
        on_device, mesh=mesh, in_specs=placed, out_specs=P(None, "ctx", "head"), check_vma=False
    )
```

```python
import jax
import jax.numpy as jnp
from jax import lax
from jax.experimental import pallas as pl
from jax.experimental.pallas import tpu as pltpu
from jax.sharding import PartitionSpec as P

HEAD_DIM = 128
BLOCK = 64
GLOB = 2
RMAX = 4
NX, NZ, NC = 4, 16, 2
ROW = NX * NC
SEQS = 4
BPD = 2
OWN = SEQS * BPD
CAP = 16
PAIRS = 4
SPLIT = 2
PART = OWN // SPLIT
MESH = pl.DeviceIdType.MESH


GROUPS = ((0, 1), (1, 3), (3, 7), (7, 11), (11, 15), (15, 16))
ROWS = OWN * BLOCK
KEYS = (3 + GLOB + RMAX) * BLOCK
NY = 4


def slot_of(d):
    return 0 if d == 0 else (2 * d - 1 if d < 8 else (15 if d == 8 else 2 * (NZ - d)))


ORDER = sorted(range(NZ), key=slot_of)


def exchange_kernel(
    q_any, k8, v8, k4, v4, w_any, req, gdist, gsel, gown, slots, counts, out, *scratch
):
    gath = [scratch[p * NZ : (p + 1) * NZ] for p in range(PAIRS)]
    rest = scratch[PAIRS * NZ :]
    cand_in, rcv, glob, win = (rest[i * PAIRS : (i + 1) * PAIRS] for i in range(4))
    (
        pack, cand, pick, req_in, req_s, q, w, weights, totals, att, att_in, partial,
        own_sem, z_send, z_recv, x_send, x_recv, c_send, c_recv, g_send, g_recv,
        h_send, h_recv, r_send, r_recv, s_sem, y_send, y_recv,
    ) = rest[4 * PAIRS :]
    ctx = lax.axis_index("ctx")
    head = lax.axis_index("head")
    x, z, c = ctx // (NZ * NC), (ctx // NC) % NZ, ctx % NC
    me = x * NC + c

    def at_z(step):
        return (x * (NZ * NC) + ((z + step + NZ) % NZ) * NC + c, head)

    def at_row(r):
        return ((r // NC) * (NZ * NC) + z * NC + r % NC, head)

    count = NX * NZ * NC
    right = ((ctx + 1) % count, head)
    left = ((ctx + count - 1) % count, head)

    own = [
        pltpu.make_async_copy(
            (k8, v8)[p % 2].at[:, :, pl.ds((p // 2) * HEAD_DIM, HEAD_DIM)],
            gath[p][0],
            own_sem.at[p],
        )
        for p in range(PAIRS)
    ]
    late = [
        pltpu.make_async_copy(
            (k4, v4)[p % 2].at[:, :, :, pl.ds((p // 2) * HEAD_DIM, HEAD_DIM)],
            win[p].at[:, pl.ds(1, BPD)],
            own_sem.at[PAIRS + p],
        )
        for p in range(PAIRS)
    ] + [
        pltpu.make_async_copy(q_any, q, own_sem.at[2 * PAIRS]),
        pltpu.make_async_copy(w_any, w, own_sem.at[2 * PAIRS + 1]),
    ]
    for copy in own:
        copy.start()
    own_req = pltpu.make_async_copy(req.at[0], req_s.at[0], s_sem.at[0])
    own_req.start()
    for copy in late:
        copy.start()

    barrier = pltpu.get_barrier_semaphore()
    peers = [at_z(1), at_z(-1), right, left] + [at_row((me + k) % ROW) for k in range(1, ROW)]
    peers += [(ctx, (head + k) % NY) for k in range(1, NY)]
    for peer in peers:
        pl.semaphore_signal(barrier, inc=1, device_id=peer, device_id_type=MESH)
    pl.semaphore_wait(barrier, len(peers))

    def req_copy(k):
        return pltpu.make_async_remote_copy(
            src_ref=req.at[k], dst_ref=req_in.at[k],
            send_sem=r_send.at[k], recv_sem=r_recv.at[k],
            device_id=at_row((me + ROW - k) % ROW), device_id_type=MESH,
        )

    for k in range(1, ROW):
        req_copy(k).start()

    def z_copy(p, way, t, a):
        if way == 0:
            src, dst, peer = (-t) % NZ, (-t - 1) % NZ, at_z(1)
        else:
            src, dst, peer = t, t + 1, at_z(-1)
        part = pl.ds(a * PART, PART)
        return pltpu.make_async_remote_copy(
            src_ref=gath[p][src].at[part],
            dst_ref=gath[p][dst].at[part],
            send_sem=z_send.at[p, (way * 8 + t) * SPLIT + a],
            recv_sem=z_recv.at[p, (way * 8 + t) * SPLIT + a],
            device_id=peer, device_id_type=MESH,
        )

    def used(way, t, a):
        return t < 7 or a // (SPLIT // 2) == way

    for copy in own:
        copy.wait()
    for a in range(SPLIT):
        for p in range(2):
            for way in range(2):
                z_copy(p, way, 0, a).start()

    halos = [
        pltpu.make_async_remote_copy(
            src_ref=(k4, v4)[p % 2].at[:, 1 - side, :, pl.ds((p // 2) * HEAD_DIM, HEAD_DIM)],
            dst_ref=win[p].at[:, 3 * side],
            send_sem=h_send.at[2 * p + side],
            recv_sem=h_recv.at[2 * p + side],
            device_id=(right, left)[side], device_id_type=MESH,
        )
        for p in range(PAIRS)
        for side in range(2)
    ]
    for copy in halos:
        copy.start()

    own_req.wait()
    for k in range(1, ROW):
        req_copy(k).wait()
    lists = [
        pltpu.make_async_copy(req_in.at[k], req_s.at[k], s_sem.at[k]) for k in range(1, ROW)
    ]
    for copy in lists:
        copy.start()
    for copy in lists:
        copy.wait()

    def x_copy(p, g, k):
        low, high = GROUPS[g]
        return pltpu.make_async_remote_copy(
            src_ref=pack.at[p, k, pl.ds(low, high - low)],
            dst_ref=rcv[p].at[pl.ds(k * CAP + low, high - low)],
            send_sem=x_send.at[p * len(GROUPS) + g, k],
            recv_sem=x_recv.at[p * len(GROUPS) + g, k],
            device_id=at_row((me + k) % ROW), device_id_type=MESH,
        )

    def c_copy(p, k):
        return pltpu.make_async_remote_copy(
            src_ref=cand.at[p, (me + k) % ROW], dst_ref=cand_in[p].at[k],
            send_sem=c_send.at[p, k], recv_sem=c_recv.at[p, k],
            device_id=at_row((me + k) % ROW), device_id_type=MESH,
        )

    def g_copy(p, k):
        return pltpu.make_async_remote_copy(
            src_ref=pick.at[p], dst_ref=glob[p].at[k],
            send_sem=g_send.at[p, k], recv_sem=g_recv.at[p, k],
            device_id=at_row((me + k) % ROW), device_id_type=MESH,
        )

    def push(p, g):
        low, high = GROUPS[g]
        for n in range(low, high):
            rcv[p][n] = gath[p][ORDER[n]][req_s[0, 0, n]]

        def fill(k, carry):
            for n in range(low, high):
                pack[p, k, n] = gath[p][ORDER[n]][req_s[k, 0, n]]
            x_copy(p, g, k).start()
            return carry

        lax.fori_loop(1, ROW, fill, 0)

    def consider(p, dists):
        def one(q, carry):
            best = cand[p, q]
            for d in dists:
                best = lax.select(gdist[q] == d, gath[p][d][gsel[q]], best)
            cand[p, q] = best
            return carry

        lax.fori_loop(0, ROW, one, 0)

    def spread(p):
        def landed(k, carry):
            c_copy(p, k).wait_recv()
            return carry

        lax.fori_loop(1, ROW, landed, 0)
        chosen = cand_in[p][gown[0]]
        pick[p] = chosen
        glob[p][0] = chosen

        def send(k, carry):
            g_copy(p, k).start()
            return carry

        lax.fori_loop(1, ROW, send, 0)

    def settle(p):
        def landed(k, carry):
            g_copy(p, k).wait_recv()
            for g in range(len(GROUPS)):
                x_copy(p, g, k).wait_recv()
            return carry

        lax.fori_loop(1, ROW, landed, 0)
        for side in range(2):
            halos[2 * p + side].wait_recv()

    def rows(p, n):
        s, j = n // BPD, n % BPD
        window = [win[p][s, j + i] for i in range(3)]
        shared = [glob[p][(me + ROW - (s * GLOB + g)) % ROW] for g in range(GLOB)]
        picked = [rcv[p][slots[n * RMAX + r]] for r in range(RMAX)]
        return jnp.concatenate(window + shared + picked, axis=0)

    column = lax.broadcasted_iota(jnp.int32, (BLOCK, KEYS), 1)

    def score(h, low, high):
        def one(n, carry):
            live = column < (3 + GLOB) * BLOCK + counts[n] * BLOCK
            scores = lax.dot_general(
                q[n, :, h * HEAD_DIM : (h + 1) * HEAD_DIM], rows(2 * h, n),
                (((1,), (1,)), ((), ())), preferred_element_type=jnp.float32,
            ) * (HEAD_DIM ** (-0.5))
            masked = jnp.where(live, scores, -1e30)
            peak = jnp.max(masked, axis=-1, keepdims=True)
            grown = jnp.where(live, jnp.exp(masked - peak), 0.0)
            weights[n] = grown.astype(jnp.bfloat16)
            totals[n] = jnp.broadcast_to(
                jnp.sum(grown, axis=-1, keepdims=True), (BLOCK, HEAD_DIM)
            )
            return carry

        lax.fori_loop(low, high, one, 0)

    def mix(h, low, high):
        def one(n, carry):
            weighted = jnp.dot(
                weights[n], rows(2 * h + 1, n), preferred_element_type=jnp.float32
            )
            at = pl.ds(pl.multiple_of(n * BLOCK, BLOCK), BLOCK)
            att[h, at, :] = (weighted / totals[n]).astype(jnp.bfloat16)
            return carry

        lax.fori_loop(low, high, one, 0)

    def y_copy(k, h, part):
        at = pl.ds(part * (ROWS // 2), ROWS // 2)
        return pltpu.make_async_remote_copy(
            src_ref=att.at[h, at], dst_ref=att_in.at[k - 1, h, at],
            send_sem=y_send.at[k, 2 * h + part], recv_sem=y_recv.at[k, 2 * h + part],
            device_id=(ctx, (head + k) % NY), device_id_type=MESH,
        )

    def share(h, part):
        for k in range(1, NY):
            y_copy(k, h, part).start()

    def compute(h, step):
        low = 2 * (step % 4)
        if step % 4 == 0:
            settle(2 * h + step // 4)
        (score, mix)[step // 4](h, low, low + 2)
        if step > 4 and step % 2:
            share(h, (step - 4) // 2)

    def one_head(h):
        both = (2 * h, 2 * h + 1)

        def first(n, carry):
            for p in both:
                cand[p, n] = gath[p][0][gsel[n]]
            return carry

        lax.fori_loop(0, ROW, first, 0)
        for t in range(1, 8):
            for a in range(SPLIT):
                for p in both:
                    for way in range(2):
                        z_copy(p, way, t - 1, a).wait_recv()
                        if used(way, t, a):
                            z_copy(p, way, t, a).start()
                        if t == 7 and h == 0:
                            z_copy(p + 2, way, 0, a).start()
                if h > 0 and t >= 4:
                    compute(h - 1, 2 * (t - 4) + a)
            for p in both:
                consider(p, (t, NZ - t))
                if t % 2:
                    push(p, (t + 1) // 2)
                if t == 3 and h > 0:
                    spread(p - 2)
        for p in both:
            for a in range(SPLIT):
                z_copy(p, a // (SPLIT // 2), 7, a).wait_recv()
            consider(p, (8,))

            def offer(k, carry, p=p):
                c_copy(p, k).start()
                return carry

            lax.fori_loop(1, ROW, offer, 0)
            cand_in[p][0] = cand[p, me]
        for p in both:
            push(p, 5)

    for p in range(PAIRS):
        push(p, 0)
    for copy in late:
        copy.wait()
    for h in range(2):
        one_head(h)
    for p in (2, 3):
        spread(p)
    for step in range(8):
        compute(1, step)

    def feature_rows(k, h):
        start = ((head + NY - k) % NY) * (2 * HEAD_DIM) + h * HEAD_DIM
        return w[pl.ds(pl.multiple_of(start, HEAD_DIM), HEAD_DIM), :]

    for k in range(1, NY):
        for part in range(2):
            y_copy(k, 0, part).wait_recv()

    def project_first(i, carry):
        at = pl.ds(pl.multiple_of(i * 128, 128), 128)
        total = jnp.dot(att[0, at, :], feature_rows(0, 0), preferred_element_type=jnp.float32)
        total += jnp.dot(att[1, at, :], feature_rows(0, 1), preferred_element_type=jnp.float32)
        for k in range(1, NY):
            total += jnp.dot(
                att_in[k - 1, 0, at, :], feature_rows(k, 0), preferred_element_type=jnp.float32
            )
        partial[at, :] = total
        return carry

    lax.fori_loop(0, ROWS // 128, project_first, 0)
    for k in range(1, NY):
        for part in range(2):
            y_copy(k, 1, part).wait_recv()

    def project_last(i, carry):
        at = pl.ds(pl.multiple_of(i * 128, 128), 128)
        total = partial[at, :]
        for k in range(1, NY):
            total += jnp.dot(
                att_in[k - 1, 1, at, :], feature_rows(k, 1), preferred_element_type=jnp.float32
            )
        out[at, :] = total.astype(jnp.bfloat16)
        return carry

    lax.fori_loop(0, ROWS // 128, project_last, 0)

    for copy in halos:
        copy.wait_send()
    for k in range(1, NY):
        for h in range(2):
            for part in range(2):
                y_copy(k, h, part).wait_send()
    for p in range(PAIRS):
        for way in range(2):
            for t in range(8):
                for a in range(SPLIT):
                    if used(way, t, a):
                        z_copy(p, way, t, a).wait_send()

        def ends(k, carry, p=p):
            c_copy(p, k).wait_send()
            g_copy(p, k).wait_send()
            for g in range(len(GROUPS)):
                x_copy(p, g, k).wait_send()
            return carry

        lax.fori_loop(1, ROW, ends, 0)


def exchange(q, keys, values, w, req, gdist, gsel, gown, slots, counts):
    width = q.shape[-1]
    block = (BLOCK, HEAD_DIM)
    dma = pltpu.SemaphoreType.DMA
    bf16 = jnp.bfloat16
    hbm = pl.BlockSpec(memory_space=pl.ANY)
    vmem = pl.BlockSpec(memory_space=pltpu.VMEM)
    smem = pl.BlockSpec(memory_space=pltpu.SMEM)
    k8, v8 = (kv.reshape(OWN, BLOCK, width) for kv in (keys, values))
    k4, v4 = (kv.reshape(SEQS, BPD, BLOCK, width) for kv in (keys, values))
    return pl.pallas_call(
        exchange_kernel,
        out_shape=jax.ShapeDtypeStruct((ROWS, w.shape[1]), bf16),
        in_specs=[hbm] * 6 + [vmem] + [smem] * 5,
        out_specs=vmem,
        scratch_shapes=[
            *([pltpu.VMEM((OWN,) + block, bf16)] * (PAIRS * NZ)),
            *([pltpu.VMEM((ROW,) + block, bf16)] * PAIRS),
            *([pltpu.VMEM((ROW * CAP,) + block, bf16)] * PAIRS),
            *([pltpu.VMEM((ROW,) + block, bf16)] * PAIRS),
            *([pltpu.VMEM((SEQS, BPD + 2) + block, bf16)] * PAIRS),
            pltpu.VMEM((PAIRS, ROW, CAP) + block, bf16),
            pltpu.VMEM((PAIRS, ROW) + block, bf16),
            pltpu.VMEM((PAIRS,) + block, bf16),
            pltpu.VMEM((ROW, 8, 128), jnp.int32),
            pltpu.SMEM((ROW, 8, 128), jnp.int32),
            pltpu.VMEM((OWN, BLOCK, width), bf16),
            pltpu.VMEM(w.shape, bf16),
            pltpu.VMEM((OWN, BLOCK, KEYS), bf16),
            pltpu.VMEM((OWN,) + block, jnp.float32),
            pltpu.VMEM((2, ROWS, HEAD_DIM), bf16),
            pltpu.VMEM((NY - 1, 2, ROWS, HEAD_DIM), bf16),
            pltpu.VMEM((ROWS, w.shape[1]), jnp.float32),
            dma((2 * PAIRS + 2,)),
            dma((PAIRS, 16 * SPLIT)), dma((PAIRS, 16 * SPLIT)),
            dma((PAIRS * len(GROUPS), ROW)), dma((PAIRS * len(GROUPS), ROW)),
            dma((PAIRS, ROW)), dma((PAIRS, ROW)),
            dma((PAIRS, ROW)), dma((PAIRS, ROW)),
            dma((2 * PAIRS,)), dma((2 * PAIRS,)),
            dma((ROW,)), dma((ROW,)),
            dma((ROW,)),
            dma((NY, 4)), dma((NY, 4)),
        ],
        compiler_params=pltpu.CompilerParams(
            collective_id=0, has_side_effects=True, vmem_limit_bytes=52 << 20
        ),
        name="exchange",
    )(q, k8, v8, k4, v4, w, req, gdist, gsel, gown, slots, counts)


def on_device(queries, keys, values, out_weight, global_ids, rand_ids, rand_count):
    seq_count, seq_rows, width = queries.shape
    q = queries.reshape(OWN, BLOCK, width)
    ctx = lax.axis_index("ctx")
    my_z = (ctx // NC) % NZ
    me = (ctx // (NZ * NC)) * NC + ctx % NC

    def place(ids, seq):
        owner = ids // BPD
        row = (owner // (NZ * NC)) * NC + owner % NC
        dist = ((owner // NC) % NZ - my_z) % NZ
        return row, dist, seq * BPD + ids % BPD

    seq_of = jnp.arange(SEQS, dtype=jnp.int32)
    row, dist, choice = place(rand_ids, seq_of[:, None, None])
    live = (jnp.arange(RMAX, dtype=jnp.int32) < rand_count[:, :, None]).reshape(-1)
    where = jnp.where(dist < 8, jnp.maximum(2 * dist - 1, 0), 2 * (NZ - dist))
    where = jnp.where(dist == 8, CAP - 1, where)
    slots = jnp.where(live, (((me - row) % ROW) * CAP + where).reshape(-1), 0)
    lane = jnp.arange(128, dtype=jnp.int32)
    place_of = jnp.arange(ROW, dtype=jnp.int32)[:, None] * CAP + lane
    hit = (place_of[:, :, None] == slots) & live & (lane < CAP)[None, :, None]
    req = jnp.max(jnp.where(hit, choice.reshape(-1), 0), axis=2)
    req = jnp.broadcast_to(req[:, None, :], (ROW, 8, 128))

    grow, gdist, gsel = place(global_ids, seq_of[:, None])
    gown = ((me - grow.reshape(-1)) % ROW)[me].reshape(1)

    return exchange(
        q, keys, values, out_weight, req, gdist.reshape(-1), gsel.reshape(-1), gown,
        slots, rand_count.reshape(-1),
    ).reshape(seq_count, seq_rows, out_weight.shape[1])


def solution(mesh):
    placed = (
        P(None, "ctx", "head"),
        P(None, "ctx", "head"),
        P(None, "ctx", "head"),
        P(None, "head"),
        P(),
        P(None, "ctx", None),
        P(None, "ctx"),
    )
    return jax.shard_map(
        on_device, mesh=mesh, in_specs=placed, out_specs=P(None, "ctx", "head"), check_vma=False
    )
```
